32 devices in a mesh: chan: 2 (over x), ket: 4 (over y, core), bra: 4 (over z).
Axes of the slice: x: 2, y: 2, z: 4, core: 2. Of those that a mesh axis runs over, the one named last changes fastest.
Arguments:
- environment: bfloat16 [16, 2048, 2048], P('chan', 'bra', 'ket'), may hold values from -6 to 6
- ket_tensor: bfloat16 [4, 2048, 2048], P(None, 'chan', 'ket'), may hold values from -0.375 to 0.375
- bra_tensor: bfloat16 [4, 2048, 2048], P(None, 'bra', 'chan'), may hold values from -0.5 to 0.5
- charge_left: int32 [2048], replicated, may hold values from 0 to 5, as said below
- charge_right: int32 [2048], replicated, may hold values from 0 to 7, as said below
- op_in: int32 [128], replicated, may hold values from 0 to 15
- op_out: int32 [128], replicated, may hold values from 0 to 15
- op_bra: int32 [128], replicated, may hold values from 0 to 3
- op_ket: int32 [128], replicated, may hold values from 0 to 3
- op_code: int32 [128], replicated, may hold values from -4 to 4
Outputs:
- new_environment: float32 [16, 2048, 2048], P('chan', 'bra', 'ket')
The draws below stay inside these ranges and needn't reach their ends.
Inputs may be any that keep to these rules, and one draw needn't show every extreme that they name: `charge_left`: charges never fall along the bond, so each charge sector is one contiguous run of states; every charge from 0 to 5 has a sector of one or more states. `charge_right`: charges never fall along the bond, so each charge sector is one contiguous run of states; every charge from 0 to 7 has a sector of one or more states.
All inputs are finite; a program needn't handle non-finite values.
Results may differ from the reference program's by a relative error of at most 0.004.
Values may be sent and summed in bfloat16 or wider, within the bound.
A program may use at most 128 MiB of HBM per device.

```python
import jax
import jax.numpy as jnp
from jax import lax

W = 16
M = 2048
MR = 2048
TERMS = 128


def sector_charges(key, count, profile):
    base = jnp.array(profile, dtype=jnp.int32)
    jitter = jax.random.randint(key, base.shape, 0, 8, dtype=jnp.int32)
    weights = base * 8 + jitter
    total = jnp.sum(weights)
    ends = jnp.cumsum(weights) * count // total
    position = jnp.arange(count, dtype=jnp.int32)
    return jnp.sum((position[:, None] >= ends[None, :-1]).astype(jnp.int32), axis=1).astype(jnp.int32)


def draw_charge_left(key, part):
    return sector_charges(jax.random.fold_in(key, 11), M, [1, 5, 8, 8, 5, 1])


def draw_charge_right(key, part):
    return sector_charges(jax.random.fold_in(key, 23), MR, [1, 3, 6, 8, 8, 6, 3, 1])


def plant(values, stream_key, low, largest):
    place = [jax.random.randint(jax.random.fold_in(stream_key, axis), (), 0, length) for axis, length in enumerate(values.shape)]
    longest = values.shape.index(max(values.shape))
    next_to = place[:longest] + [(place[longest] + 1) % values.shape[longest]] + place[longest + 1:]
    return values.at[tuple(place)].set(low).at[tuple(next_to)].set(largest)


def strengthened(entries, stream_key, source, target, parts, factor):
    def block_of(axis_at):
        return (jnp.arange(entries.shape[axis_at]) // (entries.shape[axis_at] // parts)).reshape((-1,) + (1,) * (entries.ndim - 1 - axis_at))

    near = jax.random.permutation(stream_key, parts)[block_of(target)]
    other_side = (block_of(target) + parts // 2) % parts
    return jnp.where((block_of(source) == near) | (block_of(source) == other_side), factor * entries, entries)


def shard_levels(rng, shape, pieces, least, largest):
    def one(dim, shards_of):
        heights = jax.random.uniform(jax.random.fold_in(jax.random.fold_in(rng, 6), dim), (shards_of,), jnp.float32, least / len(pieces), largest / len(pieces))
        return jnp.repeat(jnp.exp(heights), shape[dim] // shards_of).reshape((-1,) + (1,) * (len(shape) - dim - 1))

    gain = one(*pieces[0])
    for cut in pieces[1:]:
        gain = gain * one(*cut)
    return gain


def centred(key, dims, deviation, reach, split=(), held_as=jnp.bfloat16):
    loudness = shard_levels(key, dims, split, -0.22, 0.18) if split else 1.0
    values = jax.random.normal(key, dims, jnp.float32) * deviation * loudness
    return jnp.minimum(jnp.maximum(values, -reach), reach).astype(held_as)


def heavy_noise(own_key, extent, spread, bound, split, heavy, kind=jnp.bfloat16):
    values = spread * jax.random.normal(own_key, extent, jnp.float32)
    if split:
        values = values * shard_levels(own_key, extent, split, -0.22, 0.18)
    return jnp.clip(strengthened(values, jax.random.fold_in(own_key, 3), *heavy), -bound, bound).astype(kind)


def setup_inputs(seed: int = 0) -> dict:
    arg_keys = jax.random.split(jax.random.key(seed), 11)
    environment = centred(arg_keys[0], (W, M, M), 1.0, 6.0, ((0, 2), (1, 4), (2, 4)))
    ket_tensor = centred(arg_keys[1], (4, M, MR), (M // 8) ** -0.5, 0.375, ((1, 2), (2, 4)))
    bra_tensor = heavy_noise(arg_keys[2], (4, M, MR), (M // 8) ** -0.5, 0.5, ((1, 4), (2, 2)), (1, 2, 4, 2.0))
    charge_left = draw_charge_left(jax.random.fold_in(arg_keys[10], 71), 0)
    charge_right = draw_charge_right(jax.random.fold_in(arg_keys[10], 71), 0)
    op_in = plant(jax.random.randint(arg_keys[5], (TERMS,), 0, W), jax.random.fold_in(arg_keys[5], 1), 0, W - 1).astype(jnp.int32)
    op_out = plant(jax.random.randint(arg_keys[6], (TERMS,), 0, W), jax.random.fold_in(arg_keys[6], 1), 0, W - 1).astype(jnp.int32)
    op_bra = plant(jax.random.randint(arg_keys[7], (TERMS,), 0, 4), jax.random.fold_in(arg_keys[7], 1), 0, 3).astype(jnp.int32)
    op_ket = plant(jax.random.randint(arg_keys[8], (TERMS,), 0, 4), jax.random.fold_in(arg_keys[8], 1), 0, 3).astype(jnp.int32)
    op_code = plant(jax.random.randint(arg_keys[9], (TERMS,), -4, 5), jax.random.fold_in(arg_keys[9], 1), -4, 4).astype(jnp.int32)
    return dict(environment=environment, ket_tensor=ket_tensor, bra_tensor=bra_tensor, charge_left=charge_left, charge_right=charge_right, op_in=op_in, op_out=op_out, op_bra=op_bra, op_ket=op_ket, op_code=op_code)


def build_coupling(op_in, op_out, op_bra, op_ket, op_code):
    slots = jnp.arange(4 * W, dtype=jnp.int32)
    pick_in = (((op_in * 4 + op_ket)[:, None]) == slots[None, :]).astype(jnp.float32)
    pick_out = (((op_out * 4 + op_bra)[:, None]) == slots[None, :]).astype(jnp.float32)
    weights = op_code.astype(jnp.float32) * 0.25
    table = jnp.dot(pick_in.T, pick_out * weights[:, None], precision=lax.Precision.HIGHEST)
    return table.reshape(W, 4, W, 4)


def reference(environment, ket_tensor, bra_tensor, charge_left, charge_right, op_in, op_out, op_bra, op_ket, op_code):
    phys = jnp.array([0, 1, 1, 2], dtype=jnp.int32)
    allowed = (charge_left[None, :, None] + phys[:, None, None]) == charge_right[None, None, :]
    ket_masked = jnp.where(allowed, ket_tensor, jnp.zeros((), jnp.bfloat16))
    bra_masked = jnp.where(allowed, bra_tensor, jnp.zeros((), jnp.bfloat16))
    coupling = build_coupling(op_in, op_out, op_bra, op_ket, op_code)
    env_wide = environment.astype(jnp.float32)
    bra_wide = bra_masked.astype(jnp.float32)
    block = 256
    starts = jnp.arange(MR // block, dtype=jnp.int32) * block

    def one_block(start):
        ket_block = lax.dynamic_slice_in_dim(ket_masked, start, block, 2).astype(jnp.float32)
        partial_value = jnp.einsum('wbk,skq->wsbq', env_wide, ket_block, precision=lax.Precision.HIGHEST)
        partial_value = partial_value.astype(jnp.bfloat16).astype(jnp.float32)
        mixed = jnp.einsum('wsbq,wsvt->vtbq', partial_value, coupling, precision=lax.Precision.HIGHEST)
        mixed = mixed.astype(jnp.bfloat16).astype(jnp.float32)
        return jnp.einsum('tbp,vtbq->vpq', bra_wide, mixed, precision=lax.Precision.HIGHEST)

    blocks = lax.map(one_block, starts)
    return jnp.transpose(blocks, (1, 2, 0, 3)).reshape(W, MR, MR)
```

```python
import jax
import jax.numpy as jnp
from jax import lax
from jax.sharding import PartitionSpec as P

SIXTEENTHS = (3, 4, 4, 5)


def build_coupling(op_in, op_out, op_bra, op_ket, op_code, channels):
    slots = jnp.arange(4 * channels, dtype=jnp.int32)
    pick_in = ((op_in * 4 + op_ket)[:, None] == slots[None, :]).astype(jnp.float32)
    pick_out = ((op_out * 4 + op_bra)[:, None] == slots[None, :]).astype(jnp.float32)
    weights = op_code.astype(jnp.float32) * 0.25
    table = jnp.dot(pick_in.T, pick_out * weights[:, None], precision=lax.Precision.HIGHEST)
    return table.reshape(channels, 4, channels, 4)


def pack(tensor, step):
    zero = jnp.zeros((), tensor.dtype)
    first = jnp.where(
        step == 0,
        tensor[0],
        jnp.where(step == 1, tensor[1], jnp.where(step == 2, tensor[3], zero)),
    )
    return jnp.stack([first, jnp.where(step == 1, tensor[2], zero)])


def unpack(planes, step, axis):
    zero = jnp.zeros((), planes.dtype)
    first = planes[0]
    return jnp.stack(
        [
            jnp.where(step == 0, first, zero),
            jnp.where(step == 1, first, zero),
            jnp.where(step == 1, planes[1], zero),
            jnp.where(step == 2, first, zero),
        ],
        axis=axis,
    )


def gather_chan(block, axis):
    size = lax.axis_size("chan")
    if size != 2:
        return lax.all_gather(block, "chan", axis=axis, tiled=True)
    other = lax.ppermute(block, "chan", [(0, 1), (1, 0)])
    first = lax.axis_index("chan") == 0
    low = jnp.where(first, block, other)
    high = jnp.where(first, other, block)
    return jnp.concatenate([low, high], axis=axis)


def local(
    environment,
    ket_tensor,
    bra_tensor,
    charge_left,
    charge_right,
    op_in,
    op_out,
    op_bra,
    op_ket,
    op_code,
):
    n_chan = lax.axis_size("chan")
    me = lax.axis_index("chan")
    local_chan, bra_rows, ket_cols = environment.shape
    channels = local_chan * n_chan
    right_ket = ket_tensor.shape[2]
    slice_cols = right_ket // n_chan
    left_here = ket_tensor.shape[1]
    right_bra_here = bra_tensor.shape[2]
    left_all = charge_left.shape[0]
    right_all = charge_right.shape[0]
    sizes = [slice_cols * part // 16 for part in SIXTEENTHS]
    chunks = len(sizes)
    right_ket_charge = lax.dynamic_slice_in_dim(
        charge_right, lax.axis_index("ket") * right_ket, right_ket
    )
    left_bra_charge = lax.dynamic_slice_in_dim(
        charge_left, lax.axis_index("bra") * bra_rows, bra_rows
    )

    full_env = lax.all_gather(environment, "ket", axis=2, tiled=True)

    left_mine = lax.dynamic_slice_in_dim(charge_left, me * left_here, left_here)
    ket_planes = pack(ket_tensor, right_ket_charge[None, :] - left_mine[:, None])
    ket_planes = gather_chan(ket_planes, 1)
    ket_masked = unpack(
        jnp.swapaxes(ket_planes, 1, 2), right_ket_charge[:, None] - charge_left[None, :], 1
    )

    right_mine = lax.dynamic_slice_in_dim(charge_right, me * right_bra_here, right_bra_here)
    bra_planes = pack(bra_tensor, right_mine[None, :] - left_bra_charge[:, None])
    bra_planes = gather_chan(bra_planes, 2)
    bra_masked = unpack(bra_planes, charge_right[None, :] - left_bra_charge[:, None], 0)

    coupling = build_coupling(op_in, op_out, op_bra, op_ket, op_code, channels)
    coupling = coupling.reshape(n_chan, local_chan, 4, channels, 4)
    if n_chan == 2:
        coupling = jnp.where(me == 0, coupling, coupling[::-1])
    coupling = jnp.swapaxes(coupling, 1, 2).astype(jnp.bfloat16)

    def partial(ket_masked, owner, chunk):
        cols = sizes[chunk]
        start = owner * slice_cols + sum(sizes[:chunk])
        block = lax.dynamic_slice_in_dim(ket_masked, start, cols)
        value = jnp.einsum(
            "qsk,wbk->qswb", block, full_env, preferred_element_type=jnp.float32
        )
        return value.astype(jnp.bfloat16).reshape(cols, 4 * local_chan, bra_rows)

    def exchanged(chunk):
        every = jnp.stack([partial(ket_masked, owner, chunk) for owner in range(n_chan)])
        got = lax.all_to_all(every, "chan", split_axis=0, concat_axis=0, tiled=True)
        return jnp.swapaxes(got, 0, 1)

    def swap_out(summed):
        value = jnp.swapaxes(summed, 0, 1)
        parts = value.reshape((n_chan, local_chan) + value.shape[1:])
        if n_chan == 2:
            mine = lax.dynamic_index_in_dim(parts, me, 0, keepdims=False)
            theirs = lax.dynamic_index_in_dim(parts, 1 - me, 0, keepdims=False)
            away = lax.ppermute(theirs, "chan", [(0, 1), (1, 0)])
            low = jnp.where(me == 0, mine, away)
            high = jnp.where(me == 0, away, mine)
            return jnp.stack([low, high])
        return lax.all_to_all(parts, "chan", split_axis=0, concat_axis=0, tiled=True)

    if n_chan == 2:
        own, sending = partial(ket_masked, me, 0), partial(ket_masked, 1 - me, 0)
        spreads = []
        for chunk in range(chunks):
            away = lax.ppermute(sending, "chan", [(0, 1), (1, 0)])
            here = own
            if chunk + 1 < chunks:
                own = partial(ket_masked, me, chunk + 1)
                sending = partial(ket_masked, 1 - me, chunk + 1)
                away, own, sending, ket_masked = lax.optimization_barrier(
                    (away, own, sending, ket_masked)
                )
            spreads.append(jnp.stack([here, away], axis=1))
    else:
        spreads = [exchanged(chunk) for chunk in range(chunks)]
    def finish(terms, chunk):
        summed = lax.psum_scatter(terms, "bra", scatter_dimension=0, tiled=True)
        return swap_out(summed.reshape(-1, channels, sizes[chunk]))

    results = []
    for chunk in range(chunks):
        cols = sizes[chunk]
        spread = spreads[chunk]
        if chunk:
            results.append(finish(terms, chunk - 1))
            spread, _ = lax.optimization_barrier((spread, terms))
        spread = spread.reshape(cols, channels * 4, bra_rows)
        mixed = jnp.einsum(
            "qmb,mvt->qvtb",
            spread,
            coupling.reshape(channels * 4, channels, 4),
            preferred_element_type=jnp.float32,
        ).astype(jnp.bfloat16)
        terms = jnp.einsum(
            "tbp,qvtb->pvq", bra_masked, mixed, preferred_element_type=jnp.float32
        ).astype(jnp.bfloat16)
        terms = terms.reshape(right_all, channels * cols)
    results.append(finish(terms, chunks - 1))
    result = jnp.concatenate(results, axis=3)
    result = jnp.transpose(result, (1, 2, 0, 3))
    return result.reshape(local_chan, result.shape[1], right_ket).astype(jnp.float32)


def solution(mesh):
    placed = (
        P("chan", "bra", "ket"),
        P(None, "chan", "ket"),
        P(None, "bra", "chan"),
        P(),
        P(),
        P(),
        P(),
        P(),
        P(),
        P(),
    )
    return jax.shard_map(
        local, mesh=mesh, in_specs=placed, out_specs=P("chan", "bra", "ket"), check_vma=False
    )
```

```python
import jax
import jax.numpy as jnp
from jax import lax
from jax.sharding import PartitionSpec as P

SIXTEENTHS = (3, 4, 4, 5)


def build_coupling(op_in, op_out, op_bra, op_ket, op_code, channels):
    slots = jnp.arange(4 * channels, dtype=jnp.int32)
    pick_in = ((op_in * 4 + op_ket)[:, None] == slots[None, :]).astype(jnp.float32)
    pick_out = ((op_out * 4 + op_bra)[:, None] == slots[None, :]).astype(jnp.float32)
    weights = op_code.astype(jnp.float32) * 0.25
    table = jnp.dot(pick_in.T, pick_out * weights[:, None], precision=lax.Precision.HIGHEST)
    return table.reshape(channels, 4, channels, 4)


def pack(tensor, step):
    zero = jnp.zeros((), tensor.dtype)
    first = jnp.where(
        step == 0,
        tensor[0],
        jnp.where(step == 1, tensor[1], jnp.where(step == 2, tensor[3], zero)),
    )
    return jnp.stack([first, jnp.where(step == 1, tensor[2], zero)])


def unpack(planes, step, axis):
    zero = jnp.zeros((), planes.dtype)
    first = planes[0]
    return jnp.stack(
        [
            jnp.where(step == 0, first, zero),
            jnp.where(step == 1, first, zero),
            jnp.where(step == 1, planes[1], zero),
            jnp.where(step == 2, first, zero),
        ],
        axis=axis,
    )


def gather_chan(block, axis):
    size = lax.axis_size("chan")
    if size != 2:
        return lax.all_gather(block, "chan", axis=axis, tiled=True)
    other = lax.ppermute(block, "chan", [(0, 1), (1, 0)])
    first = lax.axis_index("chan") == 0
    low = jnp.where(first, block, other)
    high = jnp.where(first, other, block)
    return jnp.concatenate([low, high], axis=axis)


def local(
    environment,
    ket_tensor,
    bra_tensor,
    charge_left,
    charge_right,
    op_in,
    op_out,
    op_bra,
    op_ket,
    op_code,
):
    n_chan = lax.axis_size("chan")
    me = lax.axis_index("chan")
    local_chan, bra_rows, ket_cols = environment.shape
    channels = local_chan * n_chan
    right_ket = ket_tensor.shape[2]
    slice_cols = right_ket // n_chan
    left_here = ket_tensor.shape[1]
    right_bra_here = bra_tensor.shape[2]
    left_all = charge_left.shape[0]
    right_all = charge_right.shape[0]
    sizes = [slice_cols * part // 16 for part in SIXTEENTHS]
    chunks = len(sizes)
    right_ket_charge = lax.dynamic_slice_in_dim(
        charge_right, lax.axis_index("ket") * right_ket, right_ket
    )
    left_bra_charge = lax.dynamic_slice_in_dim(
        charge_left, lax.axis_index("bra") * bra_rows, bra_rows
    )

    full_env = lax.all_gather(environment, "ket", axis=2, tiled=True)

    left_mine = lax.dynamic_slice_in_dim(charge_left, me * left_here, left_here)
    ket_planes = pack(ket_tensor, right_ket_charge[None, :] - left_mine[:, None])
    ket_planes = gather_chan(ket_planes, 1)
    ket_masked = unpack(
        jnp.swapaxes(ket_planes, 1, 2), right_ket_charge[:, None] - charge_left[None, :], 1
    )

    right_mine = lax.dynamic_slice_in_dim(charge_right, me * right_bra_here, right_bra_here)
    bra_planes = pack(bra_tensor, right_mine[None, :] - left_bra_charge[:, None])
    bra_planes = gather_chan(bra_planes, 2)
    bra_masked = unpack(bra_planes, charge_right[None, :] - left_bra_charge[:, None], 0)

    coupling = build_coupling(op_in, op_out, op_bra, op_ket, op_code, channels)
    coupling = coupling.reshape(n_chan, local_chan, 4, channels, 4)
    if n_chan == 2:
        coupling = jnp.where(me == 0, coupling, coupling[::-1])
    coupling = jnp.swapaxes(coupling, 1, 2).astype(jnp.bfloat16)

    def partial(ket_masked, owner, chunk):
        cols = sizes[chunk]
        start = owner * slice_cols + sum(sizes[:chunk])
        block = lax.dynamic_slice_in_dim(ket_masked, start, cols)
        value = jnp.einsum(
            "qsk,wbk->qswb", block, full_env, preferred_element_type=jnp.float32
        )
        return value.astype(jnp.bfloat16).reshape(cols, 4 * local_chan, bra_rows)

    def exchanged(chunk):
        every = jnp.stack([partial(ket_masked, owner, chunk) for owner in range(n_chan)])
        got = lax.all_to_all(every, "chan", split_axis=0, concat_axis=0, tiled=True)
        return jnp.swapaxes(got, 0, 1)

    def swap_out(summed):
        value = jnp.swapaxes(summed, 0, 1)
        parts = value.reshape((n_chan, local_chan) + value.shape[1:])
        if n_chan == 2:
            mine = lax.dynamic_index_in_dim(parts, me, 0, keepdims=False)
            theirs = lax.dynamic_index_in_dim(parts, 1 - me, 0, keepdims=False)
            away = lax.ppermute(theirs, "chan", [(0, 1), (1, 0)])
            low = jnp.where(me == 0, mine, away)
            high = jnp.where(me == 0, away, mine)
            return jnp.stack([low, high])
        return lax.all_to_all(parts, "chan", split_axis=0, concat_axis=0, tiled=True)

    if n_chan == 2:
        own, sending = partial(ket_masked, me, 0), partial(ket_masked, 1 - me, 0)
        spreads = []
        for chunk in range(chunks):
            away = lax.ppermute(sending, "chan", [(0, 1), (1, 0)])
            here = own
            if chunk + 1 < chunks:
                sending = partial(ket_masked, 1 - me, chunk + 1)
                away, sending, ket_masked = lax.optimization_barrier((away, sending, ket_masked))
                own = partial(ket_masked, me, chunk + 1)
            spreads.append(jnp.stack([here, away], axis=1))
    else:
        spreads = [exchanged(chunk) for chunk in range(chunks)]
    def finish(terms, chunk):
        summed = lax.psum_scatter(terms, "bra", scatter_dimension=0, tiled=True)
        return swap_out(summed.reshape(-1, channels, sizes[chunk]))

    results = []
    for chunk in range(chunks):
        cols = sizes[chunk]
        spread = spreads[chunk]
        if chunk:
            results.append(finish(terms, chunk - 1))
            spread, _ = lax.optimization_barrier((spread, terms))
        spread = spread.reshape(cols, channels * 4, bra_rows)
        mixed = jnp.einsum(
            "qmb,mvt->qvtb",
            spread,
            coupling.reshape(channels * 4, channels, 4),
            preferred_element_type=jnp.float32,
        ).astype(jnp.bfloat16)
        terms = jnp.einsum(
            "tbp,qvtb->pvq", bra_masked, mixed, preferred_element_type=jnp.float32
        ).astype(jnp.bfloat16)
        terms = terms.reshape(right_all, channels * cols)
    results.append(finish(terms, chunks - 1))
    result = jnp.concatenate(results, axis=3)
    result = jnp.transpose(result, (1, 2, 0, 3))
    return result.reshape(local_chan, result.shape[1], right_ket).astype(jnp.float32)


def solution(mesh):
    placed = (
        P("chan", "bra", "ket"),
        P(None, "chan", "ket"),
        P(None, "bra", "chan"),
        P(),
        P(),
        P(),
        P(),
        P(),
        P(),
        P(),
    )
    return jax.shard_map(
        local, mesh=mesh, in_specs=placed, out_specs=P("chan", "bra", "ket"), check_vma=False
    )
```
